32 devices in a mesh: person: 4 (over z), variant: 8 (over y, x, core).
Axes of the slice: x: 2, y: 2, z: 4, core: 2. Of those that a mesh axis runs over, the one named last changes fastest.
Arguments:
- dosages: bfloat16 [20480, 8192], P('person', 'variant'), may hold values from -6 to 6
- phenotypes: bfloat16 [20480, 128], P(('person', 'variant')), may hold values from -16 to 16
- coefficients: float32 [8192, 128], P('variant'), may hold values from -5 to 5
- trait_precision: float32 [128], replicated, may hold values from 1 to 4
- noise: bfloat16 [8192, 128], P('variant'), may hold values from -6 to 6
- band_diag: bfloat16 [8192, 512], P('variant'), may hold values from -2 to 2
- band_lower: bfloat16 [8192, 512], P('variant'), may hold values from -0.125 to 0.125
Outputs:
- proposal: float32 [8192, 128], P('variant')
- residual: float32 [20480, 128], P(('person', 'variant'))
The draws below stay inside these ranges and needn't reach their ends.
All inputs are finite; a program needn't handle non-finite values.
Results may differ from the reference program's by a relative error of at most 0.02.
Values may be sent and summed in bfloat16 or wider, within the bound.
A program may use at most 64 MiB of HBM per device.

```python
import math
import jax
import jax.numpy as jnp
from jax import lax

K = 128
BAND = 512
P_DEV = 5120
V_DEV = 1024
P_SIZE = 20480
V = 8192
N_PERSON = 4
N_VARIANT = 8


def draw_band_diag(key, part):
    first_key, second_key = jax.random.split(jax.random.fold_in(key, 11))
    row_pos = jnp.arange(V) % BAND
    col_pos = jnp.arange(BAND)
    on_diag = row_pos[:, None] == col_pos[None, :]
    scales = jnp.exp(jax.random.uniform(first_key, (V, 1), jnp.float32, math.log(0.5), math.log(2.0)))
    off_diag = jnp.clip(jax.random.normal(second_key, (V, BAND), jnp.float32), -4.0, 4.0) * (0.4 / math.sqrt(BAND))
    return jnp.where(on_diag, scales, off_diag).astype(jnp.bfloat16)


def shard_levels(own_key, shape, cuts, low, largest):
    loudness = 1.0
    for position, shards_of in cuts:
        heights = jax.random.uniform(jax.random.fold_in(jax.random.fold_in(own_key, 6), position), (shards_of,), jnp.float32, low / len(cuts), largest / len(cuts))
        loudness = loudness * jnp.repeat(jnp.exp(heights), shape[position] // shards_of).reshape((-1,) + (1,) * (len(shape) - 1 - position))
    return loudness


def normal_values(own_key, extent, scale, most, pieces=(), kind=jnp.bfloat16):
    loudness = shard_levels(own_key, extent, pieces, -0.22, 0.18) if pieces else 1.0
    result = jax.random.normal(own_key, extent, jnp.float32) * scale * loudness
    return jnp.minimum(jnp.maximum(result, -most), most).astype(kind)


def setup_inputs(seed: int = 0) -> dict:
    key_list = jax.random.split(jax.random.key(seed), 8)
    return {
        "dosages": normal_values(key_list[0], (P_SIZE, V), 1.0, 6.0, ((0, 4), (1, 8))),
        "phenotypes": normal_values(key_list[1], (P_SIZE, K), 3.0, 16.0, ((0, 32),)),
        "coefficients": normal_values(key_list[2], (V, K), 0.7, 5.0, ((0, 8),), jnp.float32),
        "trait_precision": jnp.clip(jnp.exp(jax.random.uniform(key_list[3], (K,), jnp.float32, math.log(1.0), math.log(4.0))), 1.0, 4.0),
        "noise": normal_values(key_list[4], (V, K), 1.0, 6.0, ((0, 8),)),
        "band_diag": draw_band_diag(jax.random.fold_in(key_list[7], 71), 0),
        "band_lower": normal_values(key_list[6], (V, BAND), (4 * BAND) ** -0.5, 0.125, ((0, 8),)),
    }


step_size = 0.25

def reference(dosages, phenotypes, coefficients, trait_precision, noise, band_diag, band_lower):
    inverse_root = 1.0 / jnp.sqrt(jnp.float32(V))
    coef_half = coefficients.astype(jnp.bfloat16)
    coef_wide = coef_half.astype(jnp.float32).reshape(N_VARIANT, V_DEV, K)

    def person_step(running, person_block):
        first_row = (person_block * P_DEV).astype(jnp.int32)
        row_block = lax.dynamic_slice_in_dim(dosages, first_row, P_DEV, 0)
        targets = lax.dynamic_slice_in_dim(phenotypes, first_row, P_DEV, 0)
        dosage_wide = row_block.astype(jnp.float32).reshape(P_DEV, N_VARIANT, V_DEV)
        partial_value = jnp.einsum('pnv,nvk->pnk', dosage_wide, coef_wide)
        partial_value = lax.optimization_barrier(partial_value.astype(jnp.bfloat16)).astype(jnp.float32)
        predicted = lax.optimization_barrier(jnp.sum(partial_value, axis=1)) * inverse_root
        residual_rows = targets.astype(jnp.float32) - predicted
        resid_half = residual_rows.astype(jnp.bfloat16)
        running = running + lax.dot_general(row_block, resid_half, (((0,), (0,)), ((), ())), preferred_element_type=jnp.float32)
        return (running, residual_rows)
    blocks_index = jnp.arange(N_PERSON, dtype=jnp.int32)
    summed, residual_all = lax.scan(person_step, jnp.zeros((V, K), jnp.float32), blocks_index)
    residual = residual_all.reshape(P_SIZE, K)
    gradient = summed * inverse_root * trait_precision[None, :] - coefficients
    grad_half = lax.optimization_barrier(gradient.astype(jnp.bfloat16)).astype(jnp.float32)
    blocks = V // BAND
    diag_blocks = band_diag.astype(jnp.float32).reshape(blocks, BAND, BAND)
    lower_blocks = band_lower.astype(jnp.float32).reshape(blocks, BAND, BAND)
    grad_blocks = grad_half.reshape(blocks, BAND, K)
    own_term = jnp.einsum('bij,bik->bjk', diag_blocks, grad_blocks)
    upward = jnp.einsum('bij,bik->bjk', lower_blocks, grad_blocks)
    pulled = own_term + jnp.concatenate([upward[1:], jnp.zeros((1, BAND, K), jnp.float32)], 0)
    update = step_size / 2.0 * pulled + jnp.sqrt(jnp.float32(step_size)) * noise.astype(jnp.float32).reshape(blocks, BAND, K)
    update_half = lax.optimization_barrier(update.astype(jnp.bfloat16)).astype(jnp.float32)
    previous = jnp.concatenate([jnp.zeros((1, BAND, K), jnp.float32), update_half[:-1]], 0)
    proposal = coefficients.reshape(blocks, BAND, K) + jnp.einsum('bij,bjk->bik', diag_blocks, update_half) + jnp.einsum('bij,bjk->bik', lower_blocks, previous)
    return (proposal.reshape(V, K), residual)
```

```python
import functools
import math
import types

import jax
import jax.numpy as jnp
from jax import lax
from jax.experimental import pallas as pl
from jax.experimental.pallas import tpu as pltpu
from jax.sharding import PartitionSpec as P

step_size = 0.25
MESH = pl.DeviceIdType.MESH
CHUNKS = 4
F32 = jnp.float32
BF16 = jnp.bfloat16


def log2(n):
    return n.bit_length() - 1


def kernel(n, persons, names, x_hbm, y_hbm, coef_hbm, prec_hbm, noise_hbm, d_hbm, e_hbm, prop_hbm, res_hbm, *scratch):
    s = types.SimpleNamespace(**dict(zip(names, scratch)))
    xv, y, coef, coef_h, prec = s.x, s.y, s.coef, s.coef_h, s.prec
    d, e, noise = s.d, s.e, s.noise
    chunks, _, m, rc, variants = xv.shape
    traits = coef.shape[1]
    groups, _, cw = s.acc.shape
    blocks, _, band = s.pulled.shape
    chip_bits = log2(m)
    inverse_root = 1.0 / math.sqrt(variants * n)
    half = persons // 2

    v = lax.axis_index("variant")
    p = lax.axis_index("person")
    chip = lax.div(v, 2)
    core = v - 2 * chip
    other = 1 - core
    mate = v + 1 - 2 * core
    bit = [lax.rem(lax.div(chip, 1 << k), 2) for k in range(chip_bits)]
    weight = [other * (1 << k) + core * (1 << (chip_bits - 1 - k)) for k in range(chip_bits)]
    mine = [other * bit[k] + core * bit[chip_bits - 1 - k] for k in range(chip_bits)]
    partner = [(chip + weight[k] * (1 - 2 * mine[k])) * 2 + core for k in range(chip_bits)]

    def place(rel):
        total = 0 * chip
        for k in range(chip_bits):
            total = total + (1 - mine[k] if (rel >> k) & 1 else mine[k]) * weight[k]
        return total

    where = [place(rel) for rel in range(m)]

    def remote(src, dst, send, recv, variant=None, person=None):
        target = {"variant": variant} if person is None else {"person": person}
        return pltpu.make_async_remote_copy(
            src_ref=src, dst_ref=dst, send_sem=send, recv_sem=recv, device_id=target, device_id_type=MESH
        )

    sent = []

    def send(*args, **kw):
        copy = remote(*args, **kw)
        copy.start()
        sent.append(copy)

    loads = {}

    def load(key, src, dst):
        copy = pltpu.make_async_copy(src, dst, s.load_sem.at[len(loads)])
        copy.start()
        loads[key] = copy

    load("coef", coef_hbm, coef)
    for c in range(chunks):
        load(("x", c, 0), x_hbm.at[:, other, pl.ds(c * rc, rc), :], xv.at[c, 0])
        load(("x", c, 1), x_hbm.at[:, core, pl.ds(c * rc, rc), :], xv.at[c, 1])
    load("y", y_hbm, y)
    load("prec", prec_hbm, prec)
    load("noise", noise_hbm, noise)
    load("d", d_hbm, d)
    load("e", e_hbm, e)

    barrier = pltpu.get_barrier_semaphore()
    greeted = 1 + chip_bits
    for who in [mate] + partner:
        pl.semaphore_signal(barrier, inc=1, device_id={"variant": who}, device_id_type=MESH)

    def greet(ok, target):
        @pl.when(ok)
        def _():
            pl.semaphore_signal(barrier, inc=1, device_id=target, device_id_type=MESH)

    across = v - 1 + 2 * core
    checks = [
        (jnp.logical_and(across >= 0, across < n), {"variant": across}),
        (p > 0, {"person": p - 1}),
        (p < persons - 1, {"person": p + 1}),
    ]
    peers = greeted
    for ok, target in checks:
        greet(ok, target)
        peers = peers + ok.astype(jnp.int32)

    def barrier_wait():
        pl.semaphore_wait(barrier, peers)

    offset = [m - (m >> k) for k in range(chip_bits + 1)]

    def predict(c, t):
        loads["x", c, t].wait()
        rows = xv[c, t].reshape(m * rc, variants)
        return jnp.dot(rows, coef_h[...], preferred_element_type=F32).reshape(m, rc, traits)

    def swap(c):
        return remote(s.swap_out.at[c], s.swap_in.at[c], s.swap_send.at[c], s.swap_recv.at[c], variant=mate)

    def stage_predict(c):
        if c == 0:
            loads["coef"].wait()
            coef_h[...] = coef[...].astype(BF16)
        s.swap_out[c] = predict(c, 0).astype(BF16)
        if c == 0:
            barrier_wait()
        copy = swap(c)
        copy.start()
        sent.append(copy)
        s.sum[c] = predict(c, 1)

    def give(c, k, j, value):
        slot = offset[k] + j
        s.part_out[c, slot] = value.astype(BF16)
        send(s.part_out.at[c, slot], s.part_in.at[c, slot], s.part_send.at[c, slot],
             s.part_recv.at[c, slot], variant=partner[k])

    def finish(c, value):
        if c == 0:
            loads["y"].wait()
        rows = pl.ds(c * rc, rc)
        residual = y[rows, :].astype(F32) - value * inverse_root
        s.res[rows, :] = residual
        copy = pltpu.make_async_copy(s.res.at[rows, :], res_hbm.at[rows, :], s.out_sem.at[c])
        copy.start()
        outs.append(copy)
        s.half[c, 1, chip] = residual.astype(BF16)
        forward(c, 0)

    outs = []

    def stage_reduce(c, k):
        if k == 0:
            swap(c).wait_recv()
        count = m >> k
        order = [j for j in reversed(range(count)) if j % 2] + [j for j in reversed(range(count)) if j % 2 == 0]
        for j in order:
            spot = where[j << k]
            if k == 0:
                got = s.swap_in[c, spot]
            else:
                slot = offset[k - 1] + j
                remote(s.part_out.at[c, slot], s.part_in.at[c, slot], s.part_send.at[c, slot],
                       s.part_recv.at[c, slot], variant=partner[k - 1]).wait_recv()
                got = s.part_in[c, slot]
            value = s.sum[c, spot] + got.astype(F32)
            if k == chip_bits:
                finish(c, value)
            elif j % 2:
                give(c, k, j >> 1, value)
            else:
                s.sum[c, spot] = value

    def low(rel):
        return chip_bits if rel == 0 else (rel & -rel).bit_length() - 1

    gather_slot = {}

    def forward(c, rel):
        spot = where[rel]
        piece = s.half.at[c, 1, spot]
        for k in reversed(range(low(rel))):
            slot = gather_slot.setdefault((rel, k), len(gather_slot))
            send(piece, piece, s.half_send.at[c, slot], s.half_recv.at[c, 1, spot], variant=partner[k])
        slot = gather_slot.setdefault((rel, -1), len(gather_slot))
        send(piece, s.half.at[c, 0, spot], s.half_send.at[c, slot], s.half_recv.at[c, 0, spot], variant=mate)

    def arrived(c, t, spot, who):
        piece = s.half.at[c, t, spot]
        remote(piece, piece, s.half_send.at[c, 0], s.half_recv.at[c, t, spot], variant=who).wait_recv()

    def stage_gather(c, k):
        for rel in range(1, m):
            if low(rel) == k:
                arrived(c, 1, where[rel], partner[k])
                forward(c, rel)

    def stage_gradient(c):
        for w in range(m):
            arrived(c, 0, w, mate)
        turned = s.half[c].reshape(n * rc, traits).T
        for z in range(groups):
            cols = pl.ds(z * cw, cw)
            part = jnp.dot(turned, xv[c, :, :, :, cols].reshape(n * rc, cw), preferred_element_type=F32)
            if c:
                part = part + s.acc[z]
            s.acc[z] = part
            if c == chunks - 1:
                start_sum(z)

    side = lax.div(p, max(half, 1))
    dist = (1 - side) * (half - 1 - p) + side * (p - half)
    inward = p + 1 - 2 * side
    outward = p - 1 + 2 * side
    outer = dist < half - 1
    centre = dist == 0
    edge = dist > 0

    def to_inner(z):
        return remote(s.own.at[z], s.inner.at[z], s.inner_send.at[z], s.inner_recv.at[z], person=inward)

    def to_cross(z):
        return remote(s.own.at[z], s.cross.at[z], s.cross_send.at[z], s.cross_recv.at[z], person=inward)

    def to_outer(z):
        return remote(s.tot.at[z], s.tot.at[z], s.tot_send.at[z], s.tot_recv.at[z], person=outward)

    def send_inward(z):
        s.own[z] = s.acc[z].astype(BF16)
        @pl.when(edge)
        def _():
            to_inner(z).start()
        @pl.when(centre)
        def _():
            to_cross(z).start()

    def start_sum(z):
        if persons == 1:
            s.tot[z] = s.acc[z].astype(BF16)
            return
        @pl.when(jnp.logical_not(outer))
        def _():
            send_inward(z)

    def join_sum(z):
        @pl.when(outer)
        def _():
            to_inner(z).wait_recv()
            s.acc[z] = s.acc[z] + s.inner[z].astype(F32)
            send_inward(z)

    def cross_sum(z):
        @pl.when(centre)
        def _():
            to_cross(z).wait_recv()
            s.tot[z] = (s.own[z].astype(F32) + s.cross[z].astype(F32)).astype(BF16)
            @pl.when(outer)
            def _():
                to_outer(z).start()

    def take_sum(z):
        @pl.when(edge)
        def _():
            to_outer(z).wait_recv()
            @pl.when(outer)
            def _():
                to_outer(z).start()

    def up_copy():
        return remote(s.up_out, s.up_in, s.edge_send.at[0], s.edge_recv.at[0], variant=v - 1)

    def carry_copy():
        return remote(s.carry_out, s.carry_in, s.edge_send.at[1], s.edge_recv.at[1], variant=v + 1)

    def rows_of(j):
        return pl.ds(j * band, band)

    def block_gradient(j):
        grad = jnp.concatenate([s.grad[z] for z in range(j * band // cw, (j + 1) * band // cw)], 1)
        upward = jnp.dot(grad, e[rows_of(j), :], preferred_element_type=F32)
        if j == 0:
            @pl.when(v > 0)
            def _():
                s.up_out[...] = upward.astype(BF16)
                up_copy().start()
        else:
            s.pulled[j - 1] = s.pulled[j - 1] + upward
        s.pulled[j] = jnp.dot(grad, d[rows_of(j), :], preferred_element_type=F32)

    def block_update(j):
        value = step_size / 2.0 * s.pulled[j].T + math.sqrt(step_size) * noise[rows_of(j), :].astype(F32)
        return value.astype(BF16)

    def store_out(j):
        copy = pltpu.make_async_copy(s.prop.at[rows_of(j), :], prop_hbm.at[rows_of(j), :], s.out_sem.at[chunks + j])
        copy.start()
        outs.append(copy)

    stages = [stage_predict]
    stages += [functools.partial(stage_reduce, k=k) for k in range(chip_bits + 1)]
    stages += [functools.partial(stage_gather, k=k) for k in reversed(range(chip_bits))]
    stages += [stage_gradient]
    for slot in range(chunks + len(stages) - 1):
        for position, stage in enumerate(stages):
            if 0 <= slot - position < chunks:
                stage(slot - position)
        if slot == chunks - 1:
            loads["prec"].wait()
            spread = jnp.broadcast_to(prec[...], (traits, traits)).T
            s.prec_t[...] = spread * inverse_root
            for z in range(groups):
                s.coef_t[z] = coef[pl.ds(z * cw, cw), :].T
    for key in ("noise", "d", "e"):
        loads[key].wait()

    if persons > 1:
        for z in range(groups):
            join_sum(z)
            if z:
                cross_sum(z - 1)
        cross_sum(groups - 1)
    scale = jnp.concatenate([s.prec_t[...]] * (cw // traits), 1)
    for z in range(groups):
        if persons > 1:
            take_sum(z)
        s.grad[z] = (s.tot[z].astype(F32) * scale - s.coef_t[z]).astype(BF16)
        if (z + 1) * cw % band == 0:
            block_gradient((z + 1) * cw // band - 1)

    @pl.when(v < n - 1)
    def _():
        up_copy().wait_recv()
        s.pulled[blocks - 1] = s.pulled[blocks - 1] + s.up_in[...].astype(F32)

    s.carry_out[...] = block_update(blocks - 1)

    @pl.when(v < n - 1)
    def _():
        carry_copy().start()

    before = None
    for j in range(blocks):
        now = s.carry_out[...] if j == blocks - 1 else block_update(j)
        value = coef[rows_of(j), :] + jnp.dot(d[rows_of(j), :], now, preferred_element_type=F32)
        if j:
            value = value + jnp.dot(e[rows_of(j), :], before, preferred_element_type=F32)
        s.prop[rows_of(j), :] = value
        if j:
            store_out(j)
        before = now

    @pl.when(v > 0)
    def _():
        carry_copy().wait_recv()
        s.prop[rows_of(0), :] = s.prop[rows_of(0), :] + jnp.dot(
            e[rows_of(0), :], s.carry_in[...], preferred_element_type=F32
        )

    store_out(0)

    for copy in sent:
        copy.wait_send()
    if persons > 1:
        for z in range(groups):
            @pl.when(edge)
            def _():
                to_inner(z).wait_send()
            @pl.when(centre)
            def _():
                to_cross(z).wait_send()
            @pl.when(outer)
            def _():
                to_outer(z).wait_send()

    @pl.when(v > 0)
    def _():
        up_copy().wait_send()

    @pl.when(v < n - 1)
    def _():
        carry_copy().wait_send()

    for copy in outs:
        copy.wait()


def local(n, persons, dosages, phenotypes, coefficients, trait_precision, noise, band_diag, band_lower):
    people, variants = dosages.shape
    rows, traits = phenotypes.shape
    band = band_diag.shape[1]
    blocks = variants // band
    m = n // 2
    chunks = CHUNKS
    rc = rows // chunks
    cw = 256
    groups = variants // cw
    dma = pltpu.SemaphoreType.DMA
    scratch = dict(
        x=pltpu.VMEM((chunks, 2, m, rc, variants), BF16),
        y=pltpu.VMEM((rows, traits), BF16),
        coef=pltpu.VMEM((variants, traits), F32),
        coef_h=pltpu.VMEM((variants, traits), BF16),
        prec=pltpu.VMEM((1, traits), F32),
        noise=pltpu.VMEM((variants, traits), BF16),
        d=pltpu.VMEM((variants, band), BF16),
        e=pltpu.VMEM((variants, band), BF16),
        swap_out=pltpu.VMEM((chunks, m, rc, traits), BF16),
        swap_in=pltpu.VMEM((chunks, m, rc, traits), BF16),
        sum=pltpu.VMEM((chunks, m, rc, traits), F32),
        part_out=pltpu.VMEM((chunks, m, rc, traits), BF16),
        part_in=pltpu.VMEM((chunks, m, rc, traits), BF16),
        res=pltpu.VMEM((rows, traits), F32),
        half=pltpu.VMEM((chunks, 2, m, rc, traits), BF16),
        acc=pltpu.VMEM((groups, traits, cw), F32),
        own=pltpu.VMEM((groups, traits, cw), BF16),
        inner=pltpu.VMEM((groups, traits, cw), BF16),
        cross=pltpu.VMEM((groups, traits, cw), BF16),
        tot=pltpu.VMEM((groups, traits, cw), BF16),
        grad=pltpu.VMEM((groups, traits, cw), BF16),
        coef_t=pltpu.VMEM((groups, traits, cw), F32),
        prec_t=pltpu.VMEM((traits, traits), F32),
        pulled=pltpu.VMEM((blocks, traits, band), F32),
        up_out=pltpu.VMEM((traits, band), BF16),
        up_in=pltpu.VMEM((traits, band), BF16),
        carry_out=pltpu.VMEM((band, traits), BF16),
        carry_in=pltpu.VMEM((band, traits), BF16),
        prop=pltpu.VMEM((variants, traits), F32),
        load_sem=dma((2 * chunks + 6,)),
        swap_send=dma((chunks,)),
        swap_recv=dma((chunks,)),
        part_send=dma((chunks, m)),
        part_recv=dma((chunks, m)),
        half_send=dma((chunks, 2 * m)),
        half_recv=dma((chunks, 2, m)),
        inner_send=dma((groups,)),
        inner_recv=dma((groups,)),
        cross_send=dma((groups,)),
        cross_recv=dma((groups,)),
        tot_send=dma((groups,)),
        tot_recv=dma((groups,)),
        edge_send=dma((2,)),
        edge_recv=dma((2,)),
        out_sem=dma((chunks + blocks,)),
    )
    anywhere = pl.BlockSpec(memory_space=pl.ANY)
    return pl.pallas_call(
        functools.partial(kernel, n, persons, tuple(scratch)),
        out_shape=(
            jax.ShapeDtypeStruct((variants, traits), F32),
            jax.ShapeDtypeStruct((rows, traits), F32),
        ),
        in_specs=[anywhere] * 7,
        out_specs=(anywhere, anywhere),
        scratch_shapes=list(scratch.values()),
        compiler_params=pltpu.CompilerParams(
            collective_id=0, has_side_effects=True, vmem_limit_bytes=60 * 1024 * 1024
        ),
    )(
        dosages.reshape(m, 2, rows, variants),
        phenotypes,
        coefficients,
        trait_precision.reshape(1, traits),
        noise,
        band_diag,
        band_lower,
    )


def solution(mesh):
    n, persons = mesh.shape["variant"], mesh.shape["person"]
    placed = (
        P("person", "variant"),
        P(("person", "variant"), None),
        P("variant", None),
        P(),
        P("variant", None),
        P("variant", None),
        P("variant", None),
    )
    return jax.shard_map(
        functools.partial(local, n, persons),
        mesh=mesh,
        in_specs=placed,
        out_specs=(P("variant", None), P(("person", "variant"), None)),
        check_vma=False,
    )
```

```python
import functools
import math
import types

import jax
import jax.numpy as jnp
from jax import lax
from jax.experimental import pallas as pl
from jax.experimental.pallas import tpu as pltpu
from jax.sharding import PartitionSpec as P

step_size = 0.25
MESH = pl.DeviceIdType.MESH
CHUNKS = 4
NEAR = 1
FAR = 2
TAIL = True
GRANT = 60
GROUP = 256
F32 = jnp.float32
BF16 = jnp.bfloat16


def log2(n):
    return n.bit_length() - 1


def kernel(n, persons, names, x_hbm, y_hbm, coef_hbm, prec_hbm, noise_hbm, d_hbm, e_hbm, prop_hbm, res_hbm, *scratch):
    s = types.SimpleNamespace(**dict(zip(names, scratch)))
    xv, y, coef, coef_h, prec = s.x, s.y, s.coef, s.coef_h, s.prec
    d, e, noise = s.d, s.e, s.noise
    chunks, _, m, rc, variants = xv.shape
    traits = coef.shape[1]
    groups, _, cw = s.acc.shape
    blocks, _, band = s.pulled.shape
    chip_bits = log2(m)
    inverse_root = 1.0 / math.sqrt(variants * n)
    half = persons // 2

    v = lax.axis_index("variant")
    p = lax.axis_index("person")
    chip = lax.div(v, 2)
    core = v - 2 * chip
    other = 1 - core
    mate = v + 1 - 2 * core
    bit = [lax.rem(lax.div(chip, 1 << k), 2) for k in range(chip_bits)]
    weight = [other * (1 << k) + core * (1 << (chip_bits - 1 - k)) for k in range(chip_bits)]
    mine = [other * bit[k] + core * bit[chip_bits - 1 - k] for k in range(chip_bits)]
    partner = [(chip + weight[k] * (1 - 2 * mine[k])) * 2 + core for k in range(chip_bits)]

    def place(rel):
        total = 0 * chip
        for k in range(chip_bits):
            total = total + (1 - mine[k] if (rel >> k) & 1 else mine[k]) * weight[k]
        return total

    where = [place(rel) for rel in range(m)]

    def remote(src, dst, send, recv, variant=None, person=None):
        target = {"variant": variant} if person is None else {"person": person}
        return pltpu.make_async_remote_copy(
            src_ref=src, dst_ref=dst, send_sem=send, recv_sem=recv, device_id=target, device_id_type=MESH
        )

    sent = []

    def send(*args, **kw):
        copy = remote(*args, **kw)
        copy.start()
        sent.append(copy)

    loads = {}

    def load(key, src, dst):
        copy = pltpu.make_async_copy(src, dst, s.load_sem.at[len(loads)])
        copy.start()
        loads[key] = copy

    load("coef", coef_hbm, coef)
    for c in range(chunks):
        load(("x", c, 0), x_hbm.at[:, other, pl.ds(c * rc, rc), :], xv.at[c, 0])
        load(("x", c, 1), x_hbm.at[:, core, pl.ds(c * rc, rc), :], xv.at[c, 1])
    load("y", y_hbm, y)
    load("prec", prec_hbm, prec)
    load("noise", noise_hbm, noise)
    load("d", d_hbm, d)
    load("e", e_hbm, e)

    barrier = pltpu.get_barrier_semaphore()
    greeted = 1 + chip_bits
    for who in [mate] + partner:
        pl.semaphore_signal(barrier, inc=1, device_id={"variant": who}, device_id_type=MESH)

    def greet(ok, target):
        @pl.when(ok)
        def _():
            pl.semaphore_signal(barrier, inc=1, device_id=target, device_id_type=MESH)

    across = v - 1 + 2 * core
    checks = [
        (jnp.logical_and(across >= 0, across < n), {"variant": across}),
        (p > 0, {"person": p - 1}),
        (p < persons - 1, {"person": p + 1}),
    ]
    peers = greeted
    for ok, target in checks:
        greet(ok, target)
        peers = peers + ok.astype(jnp.int32)

    def barrier_wait():
        pl.semaphore_wait(barrier, peers)

    offset = [m - (m >> k) for k in range(chip_bits + 1)]

    def predict(c, t):
        loads["x", c, t].wait()
        rows = xv[c, t].reshape(m * rc, variants)
        return jnp.dot(rows, coef_h[...], preferred_element_type=F32).reshape(m, rc, traits)

    def swap(c):
        return remote(s.swap_out.at[c], s.swap_in.at[c], s.swap_send.at[c], s.swap_recv.at[c], variant=mate)

    def stage_predict(c):
        if c == 0:
            loads["coef"].wait()
            coef_h[...] = coef[...].astype(BF16)
        s.swap_out[c] = predict(c, 0).astype(BF16)
        if c == 0:
            barrier_wait()
        copy = swap(c)
        copy.start()
        sent.append(copy)
        s.sum[c] = predict(c, 1)

    def give(c, k, j, value):
        slot = offset[k] + j
        s.part_out[c, slot] = value.astype(BF16)
        send(s.part_out.at[c, slot], s.part_in.at[c, slot], s.part_send.at[c, slot],
             s.part_recv.at[c, slot], variant=partner[k])

    def finish(c, value):
        if c == 0:
            loads["y"].wait()
        rows = pl.ds(c * rc, rc)
        residual = y[rows, :].astype(F32) - value * inverse_root
        s.res[rows, :] = residual
        copy = pltpu.make_async_copy(s.res.at[rows, :], res_hbm.at[rows, :], s.out_sem.at[c])
        copy.start()
        outs.append(copy)
        s.half[c, 1, chip] = residual.astype(BF16)
        forward(c, 0)

    outs = []

    def stage_reduce(c, k):
        if k == 0:
            swap(c).wait_recv()
        count = m >> k
        order = [j for j in reversed(range(count)) if j % 2] + [j for j in reversed(range(count)) if j % 2 == 0]
        for j in order:
            spot = where[j << k]
            if k == 0:
                got = s.swap_in[c, spot]
            else:
                slot = offset[k - 1] + j
                remote(s.part_out.at[c, slot], s.part_in.at[c, slot], s.part_send.at[c, slot],
                       s.part_recv.at[c, slot], variant=partner[k - 1]).wait_recv()
                got = s.part_in[c, slot]
            value = s.sum[c, spot] + got.astype(F32)
            if k == chip_bits:
                finish(c, value)
            elif j % 2:
                give(c, k, j >> 1, value)
            else:
                s.sum[c, spot] = value

    def low(rel):
        return chip_bits if rel == 0 else (rel & -rel).bit_length() - 1

    gather_slot = {}

    def forward(c, rel):
        spot = where[rel]
        piece = s.half.at[c, 1, spot]
        for k in reversed(range(low(rel))):
            slot = gather_slot.setdefault((rel, k), len(gather_slot))
            send(piece, piece, s.half_send.at[c, slot], s.half_recv.at[c, 1, spot], variant=partner[k])
        slot = gather_slot.setdefault((rel, -1), len(gather_slot))
        send(piece, s.half.at[c, 0, spot], s.half_send.at[c, slot], s.half_recv.at[c, 0, spot], variant=mate)

    def arrived(c, t, spot, who):
        piece = s.half.at[c, t, spot]
        remote(piece, piece, s.half_send.at[c, 0], s.half_recv.at[c, t, spot], variant=who).wait_recv()

    def stage_gather(c, k):
        for rel in range(1, m):
            if low(rel) == k:
                arrived(c, 1, where[rel], partner[k])
                forward(c, rel)

    def stage_gradient(c):
        for w in range(m):
            arrived(c, 0, w, mate)
        turned = s.half[c].reshape(n * rc, traits).T
        for z in range(groups):
            cols = pl.ds(z * cw, cw)
            part = jnp.dot(turned, xv[c, :, :, :, cols].reshape(n * rc, cw), preferred_element_type=F32)
            if c:
                part = part + s.acc[z]
            s.acc[z] = part
            if c == chunks - 1:
                start_sum(z)

    side = lax.div(p, max(half, 1))
    dist = (1 - side) * (half - 1 - p) + side * (p - half)
    inward = p + 1 - 2 * side
    outward = p - 1 + 2 * side
    outer = dist < half - 1
    centre = dist == 0
    edge = dist > 0

    def to_inner(z):
        return remote(s.own.at[z], s.inner.at[z], s.inner_send.at[z], s.inner_recv.at[z], person=inward)

    def to_cross(z):
        return remote(s.own.at[z], s.cross.at[z], s.cross_send.at[z], s.cross_recv.at[z], person=inward)

    def to_outer(z):
        return remote(s.tot.at[z], s.tot.at[z], s.tot_send.at[z], s.tot_recv.at[z], person=outward)

    def send_inward(z):
        s.own[z] = s.acc[z].astype(BF16)
        @pl.when(edge)
        def _():
            to_inner(z).start()
        @pl.when(centre)
        def _():
            to_cross(z).start()

    def start_sum(z):
        if persons == 1:
            s.tot[z] = s.acc[z].astype(BF16)
            return
        @pl.when(jnp.logical_not(outer))
        def _():
            send_inward(z)

    def join_sum(z):
        @pl.when(outer)
        def _():
            to_inner(z).wait_recv()
            s.acc[z] = s.acc[z] + s.inner[z].astype(F32)
            send_inward(z)

    def cross_sum(z):
        @pl.when(centre)
        def _():
            to_cross(z).wait_recv()
            s.tot[z] = (s.own[z].astype(F32) + s.cross[z].astype(F32)).astype(BF16)
            @pl.when(outer)
            def _():
                to_outer(z).start()

    def take_sum(z):
        @pl.when(edge)
        def _():
            to_outer(z).wait_recv()
            @pl.when(outer)
            def _():
                to_outer(z).start()

    def up_copy():
        return remote(s.up_out, s.up_in, s.edge_send.at[0], s.edge_recv.at[0], variant=v - 1)

    def carry_copy():
        return remote(s.carry_out, s.carry_in, s.edge_send.at[1], s.edge_recv.at[1], variant=v + 1)

    def rows_of(j):
        return pl.ds(j * band, band)

    def block_gradient(j):
        grad = jnp.concatenate([s.grad[z] for z in range(j * band // cw, (j + 1) * band // cw)], 1)
        upward = jnp.dot(grad, e[rows_of(j), :], preferred_element_type=F32)
        if j == 0:
            @pl.when(v > 0)
            def _():
                s.up_out[...] = upward.astype(BF16)
                up_copy().start()
        else:
            s.pulled[j - 1] = s.pulled[j - 1] + upward
        s.pulled[j] = jnp.dot(grad, d[rows_of(j), :], preferred_element_type=F32)

    def block_update(j):
        value = step_size / 2.0 * s.pulled[j].T + math.sqrt(step_size) * noise[rows_of(j), :].astype(F32)
        return value.astype(BF16)

    def store_out(j):
        copy = pltpu.make_async_copy(s.prop.at[rows_of(j), :], prop_hbm.at[rows_of(j), :], s.out_sem.at[chunks + j])
        copy.start()
        outs.append(copy)

    stages = [stage_predict]
    stages += [functools.partial(stage_reduce, k=k) for k in range(chip_bits + 1)]
    stages += [functools.partial(stage_gather, k=k) for k in reversed(range(chip_bits))]
    stages += [stage_gradient]
    starts = [0, NEAR] + [NEAR + FAR * (k + 1) for k in range(2 * chip_bits)]
    starts.append(starts[-1] + NEAR)
    for slot in range(chunks + starts[-1]):
        for start, stage in zip(starts, stages):
            if 0 <= slot - start < chunks:
                stage(slot - start)
        if slot == chunks - 1:
            loads["prec"].wait()
            spread = jnp.broadcast_to(prec[...], (traits, traits)).T
            s.prec_t[...] = spread * inverse_root
            for z in range(groups):
                s.coef_t[z] = coef[pl.ds(z * cw, cw), :].T
    for key in ("noise", "d", "e"):
        loads[key].wait()

    if persons > 1:
        for z in range(groups):
            join_sum(z)
            if z:
                cross_sum(z - 1)
        cross_sum(groups - 1)
    scale = jnp.concatenate([s.prec_t[...]] * (cw // traits), 1)
    for z in range(groups):
        if persons > 1:
            take_sum(z)
        s.grad[z] = (s.tot[z].astype(F32) * scale - s.coef_t[z]).astype(BF16)
        if (z + 1) * cw % band == 0:
            block_gradient((z + 1) * cw // band - 1)

    @pl.when(v < n - 1)
    def _():
        up_copy().wait_recv()
        s.pulled[blocks - 1] = s.pulled[blocks - 1] + s.up_in[...].astype(F32)

    s.carry_out[...] = block_update(blocks - 1)

    @pl.when(v < n - 1)
    def _():
        carry_copy().start()

    before = None
    for j in range(blocks):
        now = s.carry_out[...] if j == blocks - 1 else block_update(j)
        value = coef[rows_of(j), :] + jnp.dot(d[rows_of(j), :], now, preferred_element_type=F32)
        if j:
            value = value + jnp.dot(e[rows_of(j), :], before, preferred_element_type=F32)
        s.prop[rows_of(j), :] = value
        if j:
            store_out(j)
        before = now

    @pl.when(v > 0)
    def _():
        carry_copy().wait_recv()
        s.prop[rows_of(0), :] = s.prop[rows_of(0), :] + jnp.dot(
            e[rows_of(0), :], s.carry_in[...], preferred_element_type=F32
        )

    store_out(0)

    for copy in sent:
        copy.wait_send()
    if persons > 1:
        for z in range(groups):
            @pl.when(edge)
            def _():
                to_inner(z).wait_send()
            @pl.when(centre)
            def _():
                to_cross(z).wait_send()
            @pl.when(outer)
            def _():
                to_outer(z).wait_send()

    @pl.when(v > 0)
    def _():
        up_copy().wait_send()

    @pl.when(v < n - 1)
    def _():
        carry_copy().wait_send()

    for copy in outs:
        copy.wait()


def hand_over(a_in, b_in, a_out, b_out, a, b, sem):
    loads = [pltpu.make_async_copy(a_in, a, sem.at[0]), pltpu.make_async_copy(b_in, b, sem.at[1])]
    stores = [pltpu.make_async_copy(a, a_out, sem.at[2]), pltpu.make_async_copy(b, b_out, sem.at[3])]
    for copy in loads:
        copy.start()
    for load, store in zip(loads, stores):
        load.wait()
        store.start()
    for copy in stores:
        copy.wait()


def local(n, persons, dosages, phenotypes, coefficients, trait_precision, noise, band_diag, band_lower):
    people, variants = dosages.shape
    rows, traits = phenotypes.shape
    band = band_diag.shape[1]
    blocks = variants // band
    m = n // 2
    chunks = CHUNKS
    rc = rows // chunks
    cw = GROUP
    groups = variants // cw
    dma = pltpu.SemaphoreType.DMA
    scratch = dict(
        x=pltpu.VMEM((chunks, 2, m, rc, variants), BF16),
        y=pltpu.VMEM((rows, traits), BF16),
        coef=pltpu.VMEM((variants, traits), F32),
        coef_h=pltpu.VMEM((variants, traits), BF16),
        prec=pltpu.VMEM((1, traits), F32),
        noise=pltpu.VMEM((variants, traits), BF16),
        d=pltpu.VMEM((variants, band), BF16),
        e=pltpu.VMEM((variants, band), BF16),
        swap_out=pltpu.VMEM((chunks, m, rc, traits), BF16),
        swap_in=pltpu.VMEM((chunks, m, rc, traits), BF16),
        sum=pltpu.VMEM((chunks, m, rc, traits), F32),
        part_out=pltpu.VMEM((chunks, m, rc, traits), BF16),
        part_in=pltpu.VMEM((chunks, m, rc, traits), BF16),
        res=pltpu.VMEM((rows, traits), F32),
        half=pltpu.VMEM((chunks, 2, m, rc, traits), BF16),
        acc=pltpu.VMEM((groups, traits, cw), F32),
        own=pltpu.VMEM((groups, traits, cw), BF16),
        inner=pltpu.VMEM((groups, traits, cw), BF16),
        cross=pltpu.VMEM((groups, traits, cw), BF16),
        tot=pltpu.VMEM((groups, traits, cw), BF16),
        grad=pltpu.VMEM((groups, traits, cw), BF16),
        coef_t=pltpu.VMEM((groups, traits, cw), F32),
        prec_t=pltpu.VMEM((traits, traits), F32),
        pulled=pltpu.VMEM((blocks, traits, band), F32),
        up_out=pltpu.VMEM((traits, band), BF16),
        up_in=pltpu.VMEM((traits, band), BF16),
        carry_out=pltpu.VMEM((band, traits), BF16),
        carry_in=pltpu.VMEM((band, traits), BF16),
        prop=pltpu.VMEM((variants, traits), F32),
        load_sem=dma((2 * chunks + 6,)),
        swap_send=dma((chunks,)),
        swap_recv=dma((chunks,)),
        part_send=dma((chunks, m)),
        part_recv=dma((chunks, m)),
        half_send=dma((chunks, 2 * m)),
        half_recv=dma((chunks, 2, m)),
        inner_send=dma((groups,)),
        inner_recv=dma((groups,)),
        cross_send=dma((groups,)),
        cross_recv=dma((groups,)),
        tot_send=dma((groups,)),
        tot_recv=dma((groups,)),
        edge_send=dma((2,)),
        edge_recv=dma((2,)),
        out_sem=dma((chunks + blocks,)),
    )
    made_shape = (
        jax.ShapeDtypeStruct((variants, traits), F32),
        jax.ShapeDtypeStruct((rows, traits), F32),
    )
    anywhere = pl.BlockSpec(memory_space=pl.ANY)
    made = pl.pallas_call(
        functools.partial(kernel, n, persons, tuple(scratch)),
        out_shape=made_shape,
        in_specs=[anywhere] * 7,
        out_specs=(anywhere, anywhere),
        scratch_shapes=list(scratch.values()),
        compiler_params=pltpu.CompilerParams(
            collective_id=0, has_side_effects=True, vmem_limit_bytes=GRANT * 1024 * 1024
        ),
    )(
        dosages.reshape(m, 2, rows, variants),
        phenotypes,
        coefficients,
        trait_precision.reshape(1, traits),
        noise,
        band_diag,
        band_lower,
    )
    if not TAIL:
        return made
    return pl.pallas_call(
        hand_over,
        out_shape=made_shape,
        in_specs=[anywhere] * 2,
        out_specs=(anywhere, anywhere),
        scratch_shapes=[
            pltpu.VMEM((variants, traits), F32),
            pltpu.VMEM((rows, traits), F32),
            dma((4,)),
        ],
        compiler_params=pltpu.CompilerParams(vmem_limit_bytes=4 * 1024 * 1024),
    )(*made)


def solution(mesh):
    n, persons = mesh.shape["variant"], mesh.shape["person"]
    placed = (
        P("person", "variant"),
        P(("person", "variant"), None),
        P("variant", None),
        P(),
        P("variant", None),
        P("variant", None),
        P("variant", None),
    )
    return jax.shard_map(
        functools.partial(local, n, persons),
        mesh=mesh,
        in_specs=placed,
        out_specs=(P("variant", None), P(("person", "variant"), None)),
        check_vma=False,
    )
```

```python
import functools
import math
import types

import jax
import jax.numpy as jnp
from jax import lax
from jax.experimental import pallas as pl
from jax.experimental.pallas import tpu as pltpu
from jax.sharding import PartitionSpec as P

step_size = 0.25
MESH = pl.DeviceIdType.MESH
CHUNKS = 4
NEAR = 1
FAR = 2
TAIL = True
GRANT = 60
GROUP = 256
F32 = jnp.float32
BF16 = jnp.bfloat16


def log2(n):
    return n.bit_length() - 1


def kernel(n, persons, names, x_hbm, y_hbm, coef_hbm, prec_hbm, noise_hbm, d_hbm, e_hbm, prop_hbm, res_hbm, *scratch):
    s = types.SimpleNamespace(**dict(zip(names, scratch)))
    xv, y, coef, coef_h, prec = s.x, s.y, s.coef, s.coef_h, s.prec
    d, e, noise = s.d, s.e, s.noise
    chunks, _, m, rc, variants = xv.shape
    traits = coef.shape[1]
    groups, _, cw = s.acc.shape
    blocks, _, band = s.pulled.shape
    chip_bits = log2(m)
    inverse_root = 1.0 / math.sqrt(variants * n)
    half = persons // 2

    v = lax.axis_index("variant")
    p = lax.axis_index("person")
    chip = lax.div(v, 2)
    core = v - 2 * chip
    other = 1 - core
    mate = v + 1 - 2 * core
    bit = [lax.rem(lax.div(chip, 1 << k), 2) for k in range(chip_bits)]
    weight = [other * (1 << k) + core * (1 << (chip_bits - 1 - k)) for k in range(chip_bits)]
    mine = [other * bit[k] + core * bit[chip_bits - 1 - k] for k in range(chip_bits)]
    partner = [(chip + weight[k] * (1 - 2 * mine[k])) * 2 + core for k in range(chip_bits)]

    def place(rel):
        total = 0 * chip
        for k in range(chip_bits):
            total = total + (1 - mine[k] if (rel >> k) & 1 else mine[k]) * weight[k]
        return total

    where = [place(rel) for rel in range(m)]

    def remote(src, dst, send, recv, variant=None, person=None):
        target = {"variant": variant} if person is None else {"person": person}
        return pltpu.make_async_remote_copy(
            src_ref=src, dst_ref=dst, send_sem=send, recv_sem=recv, device_id=target, device_id_type=MESH
        )

    sent = []

    def send(*args, **kw):
        copy = remote(*args, **kw)
        copy.start()
        sent.append(copy)

    loads = {}

    def load(key, src, dst):
        copy = pltpu.make_async_copy(src, dst, s.load_sem.at[len(loads)])
        copy.start()
        loads[key] = copy

    load("coef", coef_hbm, coef)
    for c in range(chunks):
        load(("x", c, 0), x_hbm.at[:, other, pl.ds(c * rc, rc), :], xv.at[c, 0])
        load(("x", c, 1), x_hbm.at[:, core, pl.ds(c * rc, rc), :], xv.at[c, 1])
    load("y", y_hbm, y)
    load("prec", prec_hbm, prec)
    load("noise", noise_hbm, noise)
    load("d", d_hbm, d)
    load("e", e_hbm, e)

    barrier = pltpu.get_barrier_semaphore()
    greeted = 1 + chip_bits
    for who in [mate] + partner:
        pl.semaphore_signal(barrier, inc=1, device_id={"variant": who}, device_id_type=MESH)

    def greet(ok, target):
        @pl.when(ok)
        def _():
            pl.semaphore_signal(barrier, inc=1, device_id=target, device_id_type=MESH)

    across = v - 1 + 2 * core
    checks = [
        (jnp.logical_and(across >= 0, across < n), {"variant": across}),
        (p > 0, {"person": p - 1}),
        (p < persons - 1, {"person": p + 1}),
    ]
    peers = greeted
    for ok, target in checks:
        greet(ok, target)
        peers = peers + ok.astype(jnp.int32)

    def barrier_wait():
        pl.semaphore_wait(barrier, peers)

    offset = [m - (m >> k) for k in range(chip_bits + 1)]

    def predict(c, t):
        loads["x", c, t].wait()
        rows = xv[c, t].reshape(m * rc, variants)
        return jnp.dot(rows, coef_h[...], preferred_element_type=F32).reshape(m, rc, traits)

    def swap(c):
        return remote(s.swap_out.at[c], s.swap_in.at[c], s.swap_send.at[c], s.swap_recv.at[c], variant=mate)

    def stage_predict(c):
        if c == 0:
            loads["coef"].wait()
            coef_h[...] = coef[...].astype(BF16)
        s.swap_out[c] = predict(c, 0).astype(BF16)
        if c == 0:
            barrier_wait()
        copy = swap(c)
        copy.start()
        sent.append(copy)
        s.sum[c] = predict(c, 1)

    def give(c, k, j, value):
        slot = offset[k] + j
        s.part_out[c, slot] = value.astype(BF16)
        send(s.part_out.at[c, slot], s.part_in.at[c, slot], s.part_send.at[c, slot],
             s.part_recv.at[c, slot], variant=partner[k])

    def finish(c, value):
        if c == 0:
            loads["y"].wait()
        rows = pl.ds(c * rc, rc)
        residual = y[rows, :].astype(F32) - value * inverse_root
        s.res[rows, :] = residual
        copy = pltpu.make_async_copy(s.res.at[rows, :], res_hbm.at[rows, :], s.out_sem.at[c])
        copy.start()
        outs.append(copy)
        s.half[c, 1, chip] = residual.astype(BF16)
        forward(c, 0)

    outs = []

    def stage_reduce(c, k):
        if k == 0:
            swap(c).wait_recv()
        count = m >> k
        order = [j for j in reversed(range(count)) if j % 2] + [j for j in reversed(range(count)) if j % 2 == 0]
        for j in order:
            spot = where[j << k]
            if k == 0:
                got = s.swap_in[c, spot]
            else:
                slot = offset[k - 1] + j
                remote(s.part_out.at[c, slot], s.part_in.at[c, slot], s.part_send.at[c, slot],
                       s.part_recv.at[c, slot], variant=partner[k - 1]).wait_recv()
                got = s.part_in[c, slot]
            value = s.sum[c, spot] + got.astype(F32)
            if k == chip_bits:
                finish(c, value)
            elif j % 2:
                give(c, k, j >> 1, value)
            else:
                s.sum[c, spot] = value

    def low(rel):
        return chip_bits if rel == 0 else (rel & -rel).bit_length() - 1

    gather_slot = {}

    def forward(c, rel):
        spot = where[rel]
        piece = s.half.at[c, 1, spot]
        for k in reversed(range(low(rel))):
            slot = gather_slot.setdefault((rel, k), len(gather_slot))
            send(piece, piece, s.half_send.at[c, slot], s.half_recv.at[c, 1, spot], variant=partner[k])
        slot = gather_slot.setdefault((rel, -1), len(gather_slot))
        send(piece, s.half.at[c, 0, spot], s.half_send.at[c, slot], s.half_recv.at[c, 0, spot], variant=mate)

    def arrived(c, t, spot, who):
        piece = s.half.at[c, t, spot]
        remote(piece, piece, s.half_send.at[c, 0], s.half_recv.at[c, t, spot], variant=who).wait_recv()

    def stage_gather(c, k):
        for rel in range(1, m):
            if low(rel) == k:
                arrived(c, 1, where[rel], partner[k])
                forward(c, rel)

    def stage_gradient(c):
        for w in range(m):
            arrived(c, 0, w, mate)
        turned = s.half[c].reshape(n * rc, traits).T
        for z in range(groups):
            cols = pl.ds(z * cw, cw)
            part = jnp.dot(turned, xv[c, :, :, :, cols].reshape(n * rc, cw), preferred_element_type=F32)
            if c:
                part = part + s.acc[z]
            s.acc[z] = part
            if c == chunks - 1:
                start_sum(z)

    side = lax.div(p, max(half, 1))
    dist = (1 - side) * (half - 1 - p) + side * (p - half)
    inward = p + 1 - 2 * side
    outward = p - 1 + 2 * side
    outer = dist < half - 1
    centre = dist == 0
    edge = dist > 0

    pieces = 2 * groups

    def spot(q):
        return q // 2, pl.ds((q % 2) * (traits // 2), traits // 2), slice(None)

    def to_inner(z):
        return remote(s.own.at[spot(z)], s.inner.at[spot(z)], s.inner_send.at[z], s.inner_recv.at[z], person=inward)

    def to_cross(z):
        return remote(s.own.at[spot(z)], s.cross.at[spot(z)], s.cross_send.at[z], s.cross_recv.at[z], person=inward)

    def to_outer(z):
        return remote(s.tot.at[spot(z)], s.tot.at[spot(z)], s.tot_send.at[z], s.tot_recv.at[z], person=outward)

    def send_inward(z):
        s.own[spot(z)] = s.acc[spot(z)].astype(BF16)
        @pl.when(edge)
        def _():
            to_inner(z).start()
        @pl.when(centre)
        def _():
            to_cross(z).start()

    def start_sum(z):
        if persons == 1:
            s.tot[z] = s.acc[z].astype(BF16)
            return
        @pl.when(jnp.logical_not(outer))
        def _():
            send_inward(2 * z)
            send_inward(2 * z + 1)

    def join_sum(z):
        @pl.when(outer)
        def _():
            to_inner(z).wait_recv()
            s.acc[spot(z)] = s.acc[spot(z)] + s.inner[spot(z)].astype(F32)
            send_inward(z)

    def cross_sum(z):
        @pl.when(centre)
        def _():
            to_cross(z).wait_recv()
            s.tot[spot(z)] = (s.own[spot(z)].astype(F32) + s.cross[spot(z)].astype(F32)).astype(BF16)
            @pl.when(outer)
            def _():
                to_outer(z).start()

    def take_sum(z):
        @pl.when(edge)
        def _():
            to_outer(z).wait_recv()
            @pl.when(outer)
            def _():
                to_outer(z).start()

    def up_copy():
        return remote(s.up_out, s.up_in, s.edge_send.at[0], s.edge_recv.at[0], variant=v - 1)

    def carry_copy():
        return remote(s.carry_out, s.carry_in, s.edge_send.at[1], s.edge_recv.at[1], variant=v + 1)

    def rows_of(j):
        return pl.ds(j * band, band)

    def block_gradient(j):
        grad = jnp.concatenate([s.grad[z] for z in range(j * band // cw, (j + 1) * band // cw)], 1)
        upward = jnp.dot(grad, e[rows_of(j), :], preferred_element_type=F32)
        if j == 0:
            @pl.when(v > 0)
            def _():
                s.up_out[...] = upward.astype(BF16)
                up_copy().start()
        else:
            s.pulled[j - 1] = s.pulled[j - 1] + upward
        s.pulled[j] = jnp.dot(grad, d[rows_of(j), :], preferred_element_type=F32)

    def block_update(j):
        value = step_size / 2.0 * s.pulled[j].T + math.sqrt(step_size) * noise[rows_of(j), :].astype(F32)
        return value.astype(BF16)

    def store_out(j):
        copy = pltpu.make_async_copy(s.prop.at[rows_of(j), :], prop_hbm.at[rows_of(j), :], s.out_sem.at[chunks + j])
        copy.start()
        outs.append(copy)

    stages = [stage_predict]
    stages += [functools.partial(stage_reduce, k=k) for k in range(chip_bits + 1)]
    stages += [functools.partial(stage_gather, k=k) for k in reversed(range(chip_bits))]
    stages += [stage_gradient]
    starts = [0, NEAR] + [NEAR + FAR * (k + 1) for k in range(2 * chip_bits)]
    starts.append(starts[-1] + NEAR)
    for slot in range(chunks + starts[-1]):
        for start, stage in zip(starts, stages):
            if 0 <= slot - start < chunks:
                stage(slot - start)
        if slot == chunks - 1:
            loads["prec"].wait()
            spread = jnp.broadcast_to(prec[...], (traits, traits)).T
            s.prec_t[...] = spread * inverse_root
            for z in range(groups):
                s.coef_t[z] = coef[pl.ds(z * cw, cw), :].T
    for key in ("noise", "d", "e"):
        loads[key].wait()

    if persons > 1:
        for z in range(pieces):
            join_sum(z)
            if z > 1:
                cross_sum(z - 2)
        cross_sum(pieces - 2)
        cross_sum(pieces - 1)
    scale = jnp.concatenate([s.prec_t[...]] * (cw // traits), 1)
    for z in range(groups):
        if persons > 1:
            take_sum(2 * z)
            take_sum(2 * z + 1)
        s.grad[z] = (s.tot[z].astype(F32) * scale - s.coef_t[z]).astype(BF16)
        if (z + 1) * cw % band == 0:
            block_gradient((z + 1) * cw // band - 1)

    @pl.when(v < n - 1)
    def _():
        up_copy().wait_recv()
        s.pulled[blocks - 1] = s.pulled[blocks - 1] + s.up_in[...].astype(F32)

    s.carry_out[...] = block_update(blocks - 1)

    @pl.when(v < n - 1)
    def _():
        carry_copy().start()

    before = None
    for j in range(blocks):
        now = s.carry_out[...] if j == blocks - 1 else block_update(j)
        value = coef[rows_of(j), :] + jnp.dot(d[rows_of(j), :], now, preferred_element_type=F32)
        if j:
            value = value + jnp.dot(e[rows_of(j), :], before, preferred_element_type=F32)
        s.prop[rows_of(j), :] = value
        if j:
            store_out(j)
        before = now

    @pl.when(v > 0)
    def _():
        carry_copy().wait_recv()
        s.prop[rows_of(0), :] = s.prop[rows_of(0), :] + jnp.dot(
            e[rows_of(0), :], s.carry_in[...], preferred_element_type=F32
        )

    store_out(0)

    for copy in sent:
        copy.wait_send()
    if persons > 1:
        for z in range(pieces):
            @pl.when(edge)
            def _():
                to_inner(z).wait_send()
            @pl.when(centre)
            def _():
                to_cross(z).wait_send()
            @pl.when(outer)
            def _():
                to_outer(z).wait_send()

    @pl.when(v > 0)
    def _():
        up_copy().wait_send()

    @pl.when(v < n - 1)
    def _():
        carry_copy().wait_send()

    for copy in outs:
        copy.wait()


def hand_over(a_in, b_in, a_out, b_out, a, b, sem):
    loads = [pltpu.make_async_copy(a_in, a, sem.at[0]), pltpu.make_async_copy(b_in, b, sem.at[1])]
    stores = [pltpu.make_async_copy(a, a_out, sem.at[2]), pltpu.make_async_copy(b, b_out, sem.at[3])]
    for copy in loads:
        copy.start()
    for load, store in zip(loads, stores):
        load.wait()
        store.start()
    for copy in stores:
        copy.wait()


def local(n, persons, dosages, phenotypes, coefficients, trait_precision, noise, band_diag, band_lower):
    people, variants = dosages.shape
    rows, traits = phenotypes.shape
    band = band_diag.shape[1]
    blocks = variants // band
    m = n // 2
    chunks = CHUNKS
    rc = rows // chunks
    cw = GROUP
    groups = variants // cw
    dma = pltpu.SemaphoreType.DMA
    scratch = dict(
        x=pltpu.VMEM((chunks, 2, m, rc, variants), BF16),
        y=pltpu.VMEM((rows, traits), BF16),
        coef=pltpu.VMEM((variants, traits), F32),
        coef_h=pltpu.VMEM((variants, traits), BF16),
        prec=pltpu.VMEM((1, traits), F32),
        noise=pltpu.VMEM((variants, traits), BF16),
        d=pltpu.VMEM((variants, band), BF16),
        e=pltpu.VMEM((variants, band), BF16),
        swap_out=pltpu.VMEM((chunks, m, rc, traits), BF16),
        swap_in=pltpu.VMEM((chunks, m, rc, traits), BF16),
        sum=pltpu.VMEM((chunks, m, rc, traits), F32),
        part_out=pltpu.VMEM((chunks, m, rc, traits), BF16),
        part_in=pltpu.VMEM((chunks, m, rc, traits), BF16),
        res=pltpu.VMEM((rows, traits), F32),
        half=pltpu.VMEM((chunks, 2, m, rc, traits), BF16),
        acc=pltpu.VMEM((groups, traits, cw), F32),
        own=pltpu.VMEM((groups, traits, cw), BF16),
        inner=pltpu.VMEM((groups, traits, cw), BF16),
        cross=pltpu.VMEM((groups, traits, cw), BF16),
        tot=pltpu.VMEM((groups, traits, cw), BF16),
        grad=pltpu.VMEM((groups, traits, cw), BF16),
        coef_t=pltpu.VMEM((groups, traits, cw), F32),
        prec_t=pltpu.VMEM((traits, traits), F32),
        pulled=pltpu.VMEM((blocks, traits, band), F32),
        up_out=pltpu.VMEM((traits, band), BF16),
        up_in=pltpu.VMEM((traits, band), BF16),
        carry_out=pltpu.VMEM((band, traits), BF16),
        carry_in=pltpu.VMEM((band, traits), BF16),
        prop=pltpu.VMEM((variants, traits), F32),
        load_sem=dma((2 * chunks + 6,)),
        swap_send=dma((chunks,)),
        swap_recv=dma((chunks,)),
        part_send=dma((chunks, m)),
        part_recv=dma((chunks, m)),
        half_send=dma((chunks, 2 * m)),
        half_recv=dma((chunks, 2, m)),
        inner_send=dma((2 * groups,)),
        inner_recv=dma((2 * groups,)),
        cross_send=dma((2 * groups,)),
        cross_recv=dma((2 * groups,)),
        tot_send=dma((2 * groups,)),
        tot_recv=dma((2 * groups,)),
        edge_send=dma((2,)),
        edge_recv=dma((2,)),
        out_sem=dma((chunks + blocks,)),
    )
    made_shape = (
        jax.ShapeDtypeStruct((variants, traits), F32),
        jax.ShapeDtypeStruct((rows, traits), F32),
    )
    anywhere = pl.BlockSpec(memory_space=pl.ANY)
    made = pl.pallas_call(
        functools.partial(kernel, n, persons, tuple(scratch)),
        out_shape=made_shape,
        in_specs=[anywhere] * 7,
        out_specs=(anywhere, anywhere),
        scratch_shapes=list(scratch.values()),
        compiler_params=pltpu.CompilerParams(
            collective_id=0, has_side_effects=True, vmem_limit_bytes=GRANT * 1024 * 1024
        ),
    )(
        dosages.reshape(m, 2, rows, variants),
        phenotypes,
        coefficients,
        trait_precision.reshape(1, traits),
        noise,
        band_diag,
        band_lower,
    )
    if not TAIL:
        return made
    return pl.pallas_call(
        hand_over,
        out_shape=made_shape,
        in_specs=[anywhere] * 2,
        out_specs=(anywhere, anywhere),
        scratch_shapes=[
            pltpu.VMEM((variants, traits), F32),
            pltpu.VMEM((rows, traits), F32),
            dma((4,)),
        ],
        compiler_params=pltpu.CompilerParams(vmem_limit_bytes=4 * 1024 * 1024),
    )(*made)


def solution(mesh):
    n, persons = mesh.shape["variant"], mesh.shape["person"]
    placed = (
        P("person", "variant"),
        P(("person", "variant"), None),
        P("variant", None),
        P(),
        P("variant", None),
        P("variant", None),
        P("variant", None),
    )
    return jax.shard_map(
        functools.partial(local, n, persons),
        mesh=mesh,
        in_specs=placed,
        out_specs=(P("variant", None), P(("person", "variant"), None)),
        check_vma=False,
    )
```
